512 devices in a mesh: req: 128 (over x, y_hi, z), row: 2 (over core), col: 2 (over y_lo).
Axes of the slice: x: 4, y: 8 (y_hi: 4, y_lo: 2; y = y_hi * 2 + y_lo), z: 8, core: 2. Of those that a mesh axis runs over, the one named last changes fastest.
Arguments:
- image_qkv: bfloat16 [3072, 24, 3, 1280], P(('req', 'row'), 'col'), parts along dimension 0, may hold values from -6 to 6
- text_kv: bfloat16 [12288, 2, 1280], P(('req', 'row'), None, 'col'), parts along dimension 0, may hold values from -6 to 6
- gain_query: float32 [64], replicated, may hold values from 1 to 3
- gain_key: float32 [64], replicated, may hold values from 1 to 3
- gain_text: float32 [64], replicated, may hold values from 1 to 3
- out_weight: bfloat16 [1280, 2432], P('col', 'row'), may hold values from -0.15625 to 0.15625
- final_weight: bfloat16 [64, 2432], P(None, 'row'), may hold values from -0.125 to 0.125
- hidden: bfloat16 [3072, 24, 2432], P(('req', 'row'), 'col'), parts along dimension 0, may hold values from -6 to 6
- modulation: float32 [384, 2432], P('req'), parts along dimension 0, may hold values from -3 to 3
- latent: float32 [6144, 768], P(('req', 'row'), 'col'), parts along dimension 0, may hold values from -6 to 6
- step_index: int32 [128], P('req'), parts along dimension 0, may hold values from 0 to 20
- step_count: int32 [128], P('req'), parts along dimension 0, may hold values from 1 to 5
Outputs:
- velocity: float32 [6144, 768], P(('req', 'row'), 'col'), parts along dimension 0
- latent_next: float32 [6144, 768], P(('req', 'row'), 'col'), parts along dimension 0
The draws below stay inside these ranges and needn't reach their ends.
There are 128 independent parts, one for each index of `req`. The reference program is written for one: setup_inputs(seed, part) draws one part's arguments, and reference() takes and returns one part's arrays. A program takes and returns all parts, laid end to end along the dimension named above; an argument that names none is the same for every part. Nothing has to cross between parts.
All inputs are finite; a program needn't handle non-finite values.
Results may differ from the reference program's by a relative error of at most 0.009.
Values may be sent and summed in bfloat16 or wider, within the bound.
A program may use at most 128 MiB of HBM per device.

```python
import math
import jax
import jax.numpy as jnp
from jax import lax

D = 2432
HEAD = 64
HEADS = 20
CH = 16
PATCH = 2
GRID = 24
TXT = 96
STEPS = 28
HW = 1280
LAT = 48
PATCHC = 64
N_COL = 2


def level_of(key, dims, cuts, low, largest):
    loudness, own = 1.0, jax.random.fold_in(key, 6)
    for axis_at, blocks in cuts:
        steps = jnp.exp(jax.random.uniform(jax.random.fold_in(own, axis_at), (blocks,), jnp.float32, low / len(cuts), largest / len(cuts)))
        loudness = loudness * jnp.repeat(steps, dims[axis_at] // blocks).reshape([-1 if axis == axis_at else 1 for axis in range(len(dims))])
    return loudness


def normal_values(stream_key, shape, scale, most, split=(), held_as=jnp.bfloat16):
    values = jax.random.normal(stream_key, shape, jnp.float32) * scale
    if len(split) > 0:
        values = level_of(stream_key, shape, split, -0.22, 0.18) * values
    return jnp.clip(values, min=-most, max=most).astype(held_as)


def setup_inputs(seed: int = 0, part: int = 0) -> dict:
    streams_of = jax.random.split(jax.random.key(seed), 13)
    part_keys = jax.random.split(jax.random.fold_in(streams_of[12], part), 13)
    return {
        "image_qkv": normal_values(part_keys[0], (GRID, GRID, 3, HW), 1.0, 6.0, ((0, 2), (1, 2))),
        "text_kv": normal_values(part_keys[1], (TXT, 2, HW), 1.0, 6.0, ((0, 2), (2, 2))),
        "gain_query": jnp.clip(jnp.exp(jax.random.uniform(streams_of[2], (HEAD,), jnp.float32, math.log(1.0), math.log(3.0))), 1.0, 3.0),
        "gain_key": jnp.clip(jnp.exp(jax.random.uniform(streams_of[3], (HEAD,), jnp.float32, math.log(1.0), math.log(3.0))), 1.0, 3.0),
        "gain_text": jnp.clip(jnp.exp(jax.random.uniform(streams_of[4], (HEAD,), jnp.float32, math.log(1.0), math.log(3.0))), 1.0, 3.0),
        "out_weight": normal_values(streams_of[5], (HW, D), HW ** -0.5, 0.15625, ((0, 2), (1, 2))),
        "final_weight": normal_values(streams_of[6], (PATCHC, D), D ** -0.5, 0.125, ((1, 2),)),
        "hidden": normal_values(part_keys[7], (GRID, GRID, D), 1.0, 6.0, ((0, 2), (1, 2))),
        "modulation": normal_values(part_keys[8], (3, D), 0.5, 3.0, (), jnp.float32),
        "latent": normal_values(part_keys[9], (LAT, LAT * CH), 1.0, 6.0, ((0, 2), (1, 2)), jnp.float32),
        "step_index": jax.random.randint(part_keys[10], (1,), 0, 21).astype(jnp.int32),
        "step_count": jax.random.randint(part_keys[11], (1,), 1, 6).astype(jnp.int32),
    }


SHIFT_FACTOR = 3.0

def head_rmsnorm(head_block, gain_vector):
    block_shape = head_block.shape
    width_head = gain_vector.shape[0]
    split_heads = head_block.astype(jnp.float32).reshape(block_shape[:-1] + (block_shape[-1] // width_head, width_head))
    inverse = lax.rsqrt(lax.optimization_barrier(jnp.mean(split_heads * split_heads, axis=-1, keepdims=True)) + 1e-06)
    return (split_heads * inverse * gain_vector).reshape(block_shape).astype(jnp.bfloat16)

def noise_level(step_number):
    fraction = 1.0 - step_number.astype(jnp.float32) / STEPS
    return SHIFT_FACTOR * fraction / (1.0 + (SHIFT_FACTOR - 1.0) * fraction)

def reference(image_qkv, text_kv, gain_query, gain_key, gain_text, out_weight, final_weight, hidden, modulation, latent, step_index, step_count):
    tokens_all = GRID * GRID
    queries = head_rmsnorm(image_qkv[:, :, 0], gain_query).reshape(tokens_all, HEADS, HEAD)
    key_rows = jnp.concatenate([head_rmsnorm(image_qkv[:, :, 1], gain_key).reshape(tokens_all, HEADS, HEAD), head_rmsnorm(text_kv[:, 0], gain_text).reshape(TXT, HEADS, HEAD)], axis=0)
    value_rows = jnp.concatenate([image_qkv[:, :, 2].reshape(tokens_all, HEADS, HEAD), text_kv[:, 1].reshape(TXT, HEADS, HEAD)], axis=0)
    score_scale = 1.0 / math.sqrt(HEAD)

    def single_head(operands):
        query_head, key_head, value_head = operands
        scores = jnp.dot(query_head, key_head.T, preferred_element_type=jnp.float32) * score_scale
        weights = jnp.exp(scores).astype(jnp.bfloat16)
        weighted = jnp.dot(weights, value_head, preferred_element_type=jnp.float32)
        totals = lax.optimization_barrier(jnp.sum(weights.astype(jnp.float32), axis=-1, keepdims=True))
        return (weighted / totals).astype(jnp.bfloat16)
    attended = lax.map(single_head, (queries.transpose(1, 0, 2), key_rows.transpose(1, 0, 2), value_rows.transpose(1, 0, 2)))
    attended = attended.transpose(1, 0, 2).reshape(tokens_all, HEADS * HEAD)
    group_width = HEADS * HEAD // N_COL
    projected = jnp.zeros((tokens_all, D), jnp.float32)
    for member in range(N_COL):
        product = jnp.dot(attended[:, member * group_width:(member + 1) * group_width], out_weight[member * group_width:(member + 1) * group_width], preferred_element_type=jnp.float32)
        projected = projected + lax.optimization_barrier(product.astype(jnp.bfloat16)).astype(jnp.float32)
    mixed = hidden.reshape(tokens_all, D).astype(jnp.float32) + modulation[2] * projected
    row_mean = lax.optimization_barrier(jnp.mean(mixed, axis=-1, keepdims=True))
    centered = mixed - row_mean
    row_var = lax.optimization_barrier(jnp.mean(centered * centered, axis=-1, keepdims=True))
    normed = (centered * lax.rsqrt(row_var + 1e-06) * (1.0 + modulation[1]) + modulation[0]).astype(jnp.bfloat16)
    velocity = jnp.dot(normed, final_weight.T, preferred_element_type=jnp.float32)
    velocity = velocity.reshape(GRID, GRID, PATCH, PATCH, CH).transpose(0, 2, 1, 3, 4).reshape(GRID * PATCH, GRID * PATCH * CH)
    euler_step = noise_level(step_index[0] + step_count[0]) - noise_level(step_index[0])
    return (velocity, latent + euler_step * velocity)
```

```python
import jax
import jax.numpy as jnp
from jax import lax
from jax.experimental import pallas as pl
from jax.experimental.pallas import tpu as pltpu
from jax.sharding import PartitionSpec as P

HEAD = 64
CH = 16
PATCH = 2
STEPS = 28
SHIFT_FACTOR = 3.0
EPS = 1e-06
LANES = 128
MESH = pl.DeviceIdType.MESH
F32, BF16 = jnp.float32, jnp.bfloat16


def noise_level(step_number):
    fraction = 1.0 - step_number.astype(F32) / STEPS
    return SHIFT_FACTOR * fraction / (1.0 + (SHIFT_FACTOR - 1.0) * fraction)


def block_kernel(
    qkv_hbm, text_hbm, gq_ref, gk_ref, gt_ref, wt_hbm, fw_hbm, hid_hbm, mod_hbm,
    vel_ref,
    qkv, text, hid_in, hid, mod, fw, fw_full, gains, block,
    v_out, k_out, q_out, q_own, q_peer, k_all, v_all, w_all,
    p_out, p_own, p_in,
    load_sem, send_sem, recv_sem, q_send, q_recv, p_send, p_recv,
):
    row, col = lax.axis_index("row"), lax.axis_index("col")
    to_row, to_col = {"row": 1 - row}, {"col": 1 - col}
    tile = qkv.shape[0]
    words = text.shape[0]
    width = k_all.shape[1]
    half = wt_hbm.shape[0]
    features = w_all.shape[0]
    chunk = q_send.shape[0]
    rows = tile // chunk
    pairs = width // LANES

    def load(source, target, at):
        return pltpu.make_async_copy(source, target, load_sem.at[at])

    def remote(source, target, at, device):
        return pltpu.make_async_remote_copy(
            src_ref=source, dst_ref=target, send_sem=send_sem.at[at], recv_sem=recv_sem.at[at],
            device_id=device, device_id_type=MESH,
        )

    own_half = pl.ds(pl.multiple_of(row * half, 64), half)
    load_qkv = load(qkv_hbm, qkv, 0)
    load_text = load(text_hbm, text, 1)
    load_w = load(wt_hbm, w_all.at[own_half], 2)
    load_fw = load(fw_hbm, fw.at[row], 3)
    load_hid = load(hid_hbm, hid_in, 4)
    load_mod = load(mod_hbm, mod, 5)
    load_qkv.start()
    load_text.start()
    load_w.start()
    load_fw.start()
    load_hid.start()
    load_mod.start()

    barrier = pltpu.get_barrier_semaphore()
    pl.semaphore_signal(barrier, inc=1, device_id=to_row, device_id_type=MESH)
    pl.semaphore_signal(barrier, inc=1, device_id=to_col, device_id_type=MESH)

    for at, ref in enumerate((gq_ref, gk_ref, gt_ref)):
        gains[at : at + 1, 0:HEAD] = ref[...]
        gains[at : at + 1, HEAD:LANES] = ref[...]
    down = lax.broadcasted_iota(jnp.int32, (2 * LANES, LANES), 0) // HEAD
    across = lax.broadcasted_iota(jnp.int32, (2 * LANES, LANES), 1) // HEAD
    block[...] = jnp.where(down % 2 == across, 1.0 / HEAD, 0.0).astype(BF16)

    pl.semaphore_wait(barrier, 2)

    w_copy = remote(wt_hbm, w_all.at[own_half], 0, to_row)
    fw_copy = remote(fw_hbm, fw.at[row], 1, to_row)

    def head_norm(values, gain):
        count = values.shape[0]
        pieces = [values[:, LANES * at : LANES * (at + 1)] for at in range(pairs)]
        stacked = jnp.concatenate(pieces, axis=0).astype(F32)
        square = stacked * stacked
        high = square.astype(BF16)
        low = (square - high.astype(F32)).astype(BF16)
        mean = jnp.dot(
            jnp.concatenate([high, low], axis=1), block[...], preferred_element_type=F32
        )
        normed = (stacked * lax.rsqrt(mean + EPS) * gain).astype(BF16)
        return jnp.concatenate(
            [normed[count * at : count * (at + 1)] for at in range(pairs)], axis=1
        )

    mine = pl.ds(pl.multiple_of(col * width, LANES), width)
    other = pl.ds(pl.multiple_of((1 - col) * width, LANES), width)
    own_rows, col_rows = pl.ds(0, tile), pl.ds(tile, tile)
    row_rows, far_rows = pl.ds(2 * tile, tile), pl.ds(3 * tile, tile)
    own_text, row_text = pl.ds(4 * tile, words), pl.ds(4 * tile + words, words)

    load_qkv.wait()
    v_out[...] = qkv[:, 2, other]
    v_col = remote(v_out, v_all.at[col_rows], 2, to_col)
    v_col.start()
    k_out[...] = head_norm(qkv[:, 1, other], gains[1:2])
    k_col = remote(k_out, k_all.at[col_rows], 3, to_col)
    k_col.start()
    w_copy.start()
    fw_copy.start()
    q_out[...] = head_norm(qkv[:, 0, other], gains[0:1] * 0.125)

    def q_copy(at):
        part = pl.ds(pl.multiple_of(at * rows, 16), rows)
        return pltpu.make_async_remote_copy(
            src_ref=q_out.at[part], dst_ref=q_peer.at[part],
            send_sem=q_send.at[at], recv_sem=q_recv.at[at],
            device_id=to_col, device_id_type=MESH,
        )

    for at in range(chunk):
        q_copy(at).start()

    v_all[own_rows, :] = qkv[:, 2, mine]
    v_row = remote(v_all.at[own_rows], v_all.at[row_rows], 4, to_row)
    v_row.start()
    k_all[own_rows, :] = head_norm(qkv[:, 1, mine], gains[1:2])
    k_row = remote(k_all.at[own_rows], k_all.at[row_rows], 5, to_row)
    k_row.start()
    load_text.wait()
    v_all[own_text, :] = text[:, 1, :]
    vt_row = remote(v_all.at[own_text], v_all.at[row_text], 6, to_row)
    vt_row.start()
    k_all[own_text, :] = head_norm(text[:, 0, :], gains[2:3])
    kt_row = remote(k_all.at[own_text], k_all.at[row_text], 7, to_row)
    kt_row.start()
    q_own[...] = head_norm(qkv[:, 0, mine], gains[0:1] * 0.125)

    load_hid.wait()
    grid_cols = hid_in.shape[1]
    for at in range(hid_in.shape[0]):
        hid[grid_cols * at : grid_cols * (at + 1), :] = hid_in[at]

    v_col.wait_recv()
    v_far = remote(v_all.at[col_rows], v_all.at[far_rows], 8, to_row)
    v_far.start()
    load_fw.wait()
    fw_copy.wait()
    fw_full[:, 0:half] = fw[0]
    fw_full[:, half:features] = fw[1]
    k_col.wait_recv()
    k_far = remote(k_all.at[col_rows], k_all.at[far_rows], 9, to_row)
    k_far.start()
    load_w.wait()
    w_copy.wait()
    load_mod.wait()
    v_row.wait()
    k_row.wait()
    vt_row.wait()
    kt_row.wait()
    v_far.wait()
    k_far.wait()

    low_half = lax.broadcasted_iota(jnp.int32, (rows, LANES), 1) < HEAD
    ones = jnp.ones((k_all.shape[0], LANES), BF16)

    def attend(queries):
        parts = []
        for at in range(pairs):
            lanes = slice(LANES * at, LANES * (at + 1))
            pair = queries[:, lanes].astype(F32)
            both = jnp.concatenate(
                [jnp.where(low_half, pair, 0.0), jnp.where(low_half, 0.0, pair)], axis=0
            ).astype(BF16)
            scores = lax.dot_general(
                both, k_all[:, lanes], (((1,), (1,)), ((), ())), preferred_element_type=F32
            )
            weights = jnp.exp(scores).astype(BF16)
            sums = jnp.dot(
                weights, jnp.concatenate([v_all[:, lanes], ones], axis=1),
                preferred_element_type=F32,
            )
            weighted = jnp.where(low_half, sums[:rows, :LANES], sums[rows:, :LANES])
            totals = jnp.where(low_half, sums[:rows, LANES:], sums[rows:, LANES:])
            parts.append((weighted / totals).astype(BF16))
        return jnp.concatenate(parts, axis=1)

    def project(attended):
        return lax.dot_general(
            attended, w_all[...], (((1,), (1,)), ((), ())), preferred_element_type=F32
        ).astype(BF16)

    def p_copy(at):
        part = pl.ds(pl.multiple_of(at * rows, 16), rows)
        return pltpu.make_async_remote_copy(
            src_ref=p_out.at[part], dst_ref=p_in.at[part],
            send_sem=p_send.at[at], recv_sem=p_recv.at[at],
            device_id=to_col, device_id_type=MESH,
        )

    @pl.loop(0, chunk)
    def _(at):
        part = pl.ds(pl.multiple_of(at * rows, 16), rows)
        q_copy(at).wait_recv()
        p_out[part, :] = project(attend(q_peer[part, :]))
        p_copy(at).start()

    @pl.loop(0, chunk)
    def _(at):
        part = pl.ds(pl.multiple_of(at * rows, 16), rows)
        p_own[part, :] = project(attend(q_own[part, :]))

    @pl.loop(0, chunk)
    def _(at):
        part = pl.ds(pl.multiple_of(at * rows, 16), rows)
        p_copy(at).wait_recv()
        projected = p_own[part, :].astype(F32) + p_in[part, :].astype(F32)
        mixed = hid[part, :].astype(F32) + mod[2:3, :] * projected
        mean = jnp.sum(mixed, axis=-1, keepdims=True) * (1.0 / features)
        centered = mixed - mean
        var = jnp.sum(centered * centered, axis=-1, keepdims=True) * (1.0 / features)
        normed = centered * lax.rsqrt(var + EPS) * (1.0 + mod[1:2, :]) + mod[0:1, :]
        vel_ref[part, :] = lax.dot_general(
            normed.astype(BF16), fw_full[...], (((1,), (1,)), ((), ())),
            preferred_element_type=F32,
        )

    v_col.wait_send()
    k_col.wait_send()

    @pl.loop(0, chunk)
    def _(at):
        q_copy(at).wait_send()
        p_copy(at).wait_send()


def on_device(
    image_qkv, text_kv, gain_query, gain_key, gain_text, out_weight, final_weight,
    hidden, modulation, latent, step_index, step_count,
):
    tile_rows, tile_cols, _, heads_width = image_qkv.shape
    tile = tile_rows * tile_cols
    words, _, width = text_kv.shape
    half = out_weight.shape[1]
    features = hidden.shape[2]
    patch_values = final_weight.shape[0]
    keys = 4 * tile + 2 * words
    chunk = 3
    anywhere = pl.BlockSpec(memory_space=pl.ANY)
    vmem = pl.BlockSpec(memory_space=pltpu.VMEM)
    velocity = pl.pallas_call(
        block_kernel,
        out_shape=jax.ShapeDtypeStruct((tile, patch_values), F32),
        in_specs=[anywhere, anywhere, vmem, vmem, vmem, anywhere, anywhere, anywhere, anywhere],
        out_specs=vmem,
        scratch_shapes=[
            pltpu.VMEM((tile, 3, heads_width), BF16),
            pltpu.VMEM((words, 2, width), BF16),
            pltpu.VMEM((tile_rows, tile_cols, features), BF16),
            pltpu.VMEM((tile, features), BF16),
            pltpu.VMEM((3, features), F32),
            pltpu.VMEM((2, patch_values, half), BF16),
            pltpu.VMEM((patch_values, features), BF16),
            pltpu.VMEM((8, LANES), F32),
            pltpu.VMEM((2 * LANES, LANES), BF16),
            pltpu.VMEM((tile, width), BF16),
            pltpu.VMEM((tile, width), BF16),
            pltpu.VMEM((tile, width), BF16),
            pltpu.VMEM((tile, width), BF16),
            pltpu.VMEM((tile, width), BF16),
            pltpu.VMEM((keys, width), BF16),
            pltpu.VMEM((keys, width), BF16),
            pltpu.VMEM((features, width), BF16),
            pltpu.VMEM((tile, features), BF16),
            pltpu.VMEM((tile, features), BF16),
            pltpu.VMEM((tile, features), BF16),
            pltpu.SemaphoreType.DMA((6,)),
            pltpu.SemaphoreType.DMA((10,)),
            pltpu.SemaphoreType.DMA((10,)),
            pltpu.SemaphoreType.DMA((chunk,)),
            pltpu.SemaphoreType.DMA((chunk,)),
            pltpu.SemaphoreType.DMA((chunk,)),
            pltpu.SemaphoreType.DMA((chunk,)),
        ],
        compiler_params=pltpu.CompilerParams(
            collective_id=0, has_side_effects=True
        ),
        name="attention_block",
    )(
        image_qkv.reshape(tile, 3, heads_width), text_kv,
        gain_query.reshape(1, HEAD), gain_key.reshape(1, HEAD), gain_text.reshape(1, HEAD),
        out_weight.T, final_weight, hidden, modulation,
    )
    velocity = (
        velocity.reshape(tile_rows, tile_cols, PATCH, PATCH, CH)
        .transpose(0, 2, 1, 3, 4)
        .reshape(tile_rows * PATCH, tile_cols * PATCH * CH)
    )
    euler_step = noise_level(step_index[0] + step_count[0]) - noise_level(step_index[0])
    return (velocity, latent + euler_step * velocity)


def solution(mesh):
    placed = (
        P(("req", "row"), "col", None, None),
        P(("req", "row"), None, "col"),
        P(),
        P(),
        P(),
        P("col", "row"),
        P(None, "row"),
        P(("req", "row"), "col", None),
        P("req", None),
        P(("req", "row"), "col"),
        P("req"),
        P("req"),
    )
    return jax.shard_map(
        on_device,
        mesh=mesh,
        in_specs=placed,
        out_specs=(P(("req", "row"), "col"), P(("req", "row"), "col")),
        check_vma=False,
    )
```

```python
import functools

import jax
import jax.numpy as jnp
from jax import lax
from jax.experimental import pallas as pl
from jax.experimental.pallas import tpu as pltpu
from jax.sharding import PartitionSpec as P

HEAD = 64
CH = 16
PATCH = 2
STEPS = 28
SHIFT_FACTOR = 3.0
EPS = 1e-06
LANES = 128
TORUS = (4, 4, 8)
MESH = pl.DeviceIdType.MESH
F32, BF16 = jnp.float32, jnp.bfloat16


def noise_level(step_number):
    fraction = 1.0 - step_number.astype(F32) / STEPS
    return SHIFT_FACTOR * fraction / (1.0 + (SHIFT_FACTOR - 1.0) * fraction)


def block_kernel(
    torus,
    qkv_hbm, text_hbm, gq_ref, gk_ref, gt_ref, wt_hbm, fw_hbm, hid_hbm, mod_hbm,
    vel_ref,
    qkv, text, hid_in, hid, mod, fw, fw_full, gains, block,
    v_out, k_out, q_out, q_all, k_all, v_all, w_own, w_oth,
    att_out, att_in, att_own, p_own, p_oth,
    load_sem, send_sem, recv_sem, pair_send, pair_recv, w_send, w_recv,
):
    row, col = lax.axis_index("row"), lax.axis_index("col")
    to_row, to_col = {"row": 1 - row}, {"col": 1 - col}
    tile = qkv.shape[0]
    words = text.shape[0]
    pairs, keys, _ = k_all.shape
    width = pairs * LANES
    half = wt_hbm.shape[0]
    features = w_own.shape[0]

    def load(source, target, at):
        return pltpu.make_async_copy(source, target, load_sem.at[at])

    def remote(source, target, sems, at, device):
        return pltpu.make_async_remote_copy(
            src_ref=source, dst_ref=target, send_sem=sems[0].at[at], recv_sem=sems[1].at[at],
            device_id=device, device_id_type=MESH,
        )

    plain, paired, weight = (send_sem, recv_sem), (pair_send, pair_recv), (w_send, w_recv)

    own_half = pl.ds(pl.multiple_of(row * half, 64), half)
    load_qkv = load(qkv_hbm, qkv, 0)
    load_text = load(text_hbm, text, 1)
    load_w = load(wt_hbm, w_own.at[own_half], 2)
    load_fw = load(fw_hbm, fw.at[row], 3)
    load_hid = load(hid_hbm, hid_in, 4)
    load_mod = load(mod_hbm, mod, 5)
    load_qkv.start()
    load_text.start()
    load_w.start()
    load_fw.start()
    load_hid.start()
    load_mod.start()

    partners = [to_row, to_col]
    if torus:
        size_x, size_y, size_z = torus
        req = lax.axis_index("req")
        at_z = req % size_z
        at_y = (req // size_z) % size_y
        at_x = req // (size_z * size_y)

        def chip(x, y, z):
            return ((x % size_x) * size_y + y % size_y) * size_z + z % size_z

        to_y = {"req": chip(at_x, at_y + size_y + 2 * col - 1, at_z), "col": 1 - col}
        to_x = [{"req": chip(at_x + step, at_y, at_z)} for step in (1, size_x - 1)]
        to_z = [{"req": chip(at_x, at_y, at_z + step)} for step in (1, size_z - 1)]
        partners += [to_y, *to_x, *to_z]

    barrier = pltpu.get_barrier_semaphore()
    for partner in partners:
        pl.semaphore_signal(barrier, inc=1, device_id=partner, device_id_type=MESH)

    for at, ref in enumerate((gq_ref, gk_ref, gt_ref)):
        gains[at : at + 1, 0:HEAD] = ref[...]
        gains[at : at + 1, HEAD:LANES] = ref[...]
    down = lax.broadcasted_iota(jnp.int32, (2 * LANES, LANES), 0) // HEAD
    across = lax.broadcasted_iota(jnp.int32, (2 * LANES, LANES), 1) // HEAD
    block[...] = jnp.where(down % 2 == across, 1.0 / HEAD, 0.0).astype(BF16)

    pl.semaphore_wait(barrier, len(partners))

    if torus:
        quarter = half // 4
        first = quarter // 32 * 16 + 16
        parts = ((0, first), (first, quarter - first))
        colour = (at_x + 2 * at_z) % 4

        def piece(which, part, base):
            start, count = parts[part]
            offset = base + (which % 4) * quarter + start
            return pl.ds(pl.multiple_of(offset, 16), count)

        def near(part):
            return remote(
                wt_hbm.at[piece(colour, part, 0)],
                w_oth.at[piece(colour, part, row * half)], weight, part, to_y,
            )

        def spread(which, part, at, device):
            rows = piece(which, part, row * half)
            return remote(w_oth.at[rows], w_oth.at[rows], weight, at, device)

        def across_x(part, side, which):
            return spread(which, part, 2 + 2 * side + part, to_x[side])

        def across_z(part, which):
            return spread(which, part, 6 + part, to_z[part])

        def across_row(which, part, at):
            return spread(which, part, at, to_row)

        near(0).start()
        near(1).start()
    else:
        near = remote(wt_hbm, w_oth.at[own_half], weight, 0, to_col)
    w_row = remote(wt_hbm, w_own.at[own_half], plain, 0, to_row)
    fw_row = remote(fw_hbm, fw.at[row], plain, 1, to_row)

    def head_norm(values, gain):
        count = values.shape[0]
        pieces = [values[:, LANES * at : LANES * (at + 1)] for at in range(pairs)]
        stacked = jnp.concatenate(pieces, axis=0).astype(F32)
        square = stacked * stacked
        high = square.astype(BF16)
        low = (square - high.astype(F32)).astype(BF16)
        mean = jnp.dot(
            jnp.concatenate([high, low], axis=1), block[...], preferred_element_type=F32
        )
        normed = (stacked * lax.rsqrt(mean + EPS) * gain).astype(BF16)
        return normed.reshape(pairs, count, LANES)

    def split(values):
        return [values[:, LANES * at : LANES * (at + 1)] for at in range(pairs)]

    mine = pl.ds(pl.multiple_of(col * width, LANES), width)
    other = pl.ds(pl.multiple_of((1 - col) * width, LANES), width)
    own_rows, col_rows = pl.ds(0, tile), pl.ds(tile, tile)
    row_rows, far_rows = pl.ds(2 * tile, tile), pl.ds(3 * tile, tile)
    own_text, row_text = pl.ds(4 * tile, words), pl.ds(4 * tile + words, words)

    def k_col(at):
        return remote(k_out.at[at], k_all.at[at, col_rows], paired, at, to_col)

    def v_col(at):
        return remote(v_out.at[at], v_all.at[at, col_rows], paired, pairs + at, to_col)

    def q_col(at):
        return remote(q_out.at[at], q_all.at[at, own_rows], paired, 2 * pairs + at, to_col)

    def k_far(at):
        return remote(
            k_all.at[at, col_rows], k_all.at[at, far_rows], paired, 3 * pairs + at, to_row
        )

    def v_far(at):
        return remote(
            v_all.at[at, col_rows], v_all.at[at, far_rows], paired, 4 * pairs + at, to_row
        )

    def att_col(at):
        return remote(att_out.at[at], att_in.at[at], paired, 5 * pairs + at, to_col)

    load_qkv.wait()
    for at, part in enumerate(split(qkv[:, 2, other])):
        v_out[at] = part
    v_col(0).start()
    v_col(1).start()
    k_out[...] = head_norm(qkv[:, 1, other], gains[1:2])
    k_col(0).start()
    q_out[...] = head_norm(qkv[:, 0, other], gains[0:1] * 0.125)
    q_col(0).start()
    k_col(1).start()
    q_col(1).start()
    for at in range(2, pairs):
        k_col(at).start()
        v_col(at).start()
        q_col(at).start()

    for at, part in enumerate(split(qkv[:, 2, mine])):
        v_all[at, own_rows, :] = part
    v_row = remote(v_all.at[:, own_rows], v_all.at[:, row_rows], plain, 2, to_row)
    v_row.start()
    k_all[:, own_rows, :] = head_norm(qkv[:, 1, mine], gains[1:2])
    k_row = remote(k_all.at[:, own_rows], k_all.at[:, row_rows], plain, 3, to_row)
    k_row.start()
    load_text.wait()
    for at, part in enumerate(split(text[:, 1, :])):
        v_all[at, own_text, :] = part
    vt_row = remote(v_all.at[:, own_text], v_all.at[:, row_text], plain, 4, to_row)
    vt_row.start()
    k_all[:, own_text, :] = head_norm(text[:, 0, :], gains[2:3])
    kt_row = remote(k_all.at[:, own_text], k_all.at[:, row_text], plain, 5, to_row)
    kt_row.start()
    w_row.start()
    fw_row.start()
    if not torus:
        near.start()
    q_all[:, col_rows, :] = head_norm(qkv[:, 0, mine], gains[0:1] * 0.125)

    def spread_near(part):
        near(part).wait_recv()
        across_x(part, 0, colour).start()
        across_x(part, 1, colour).start()
        across_z(part, colour).start()
        across_row(colour, part, 8 + part).start()

    v_row.wait()
    k_row.wait()
    vt_row.wait()
    kt_row.wait()

    low_half = lax.broadcasted_iota(jnp.int32, (tile, LANES), 1) < HEAD
    ones = jnp.ones((keys, LANES), BF16)

    def attend(at, rows):
        pair = q_all[at, rows, :].astype(F32)
        both = jnp.concatenate(
            [jnp.where(low_half, pair, 0.0), jnp.where(low_half, 0.0, pair)], axis=0
        ).astype(BF16)
        scores = lax.dot_general(
            both, k_all[at], (((1,), (1,)), ((), ())), preferred_element_type=F32
        )
        weights = jnp.exp(scores).astype(BF16)
        sums = jnp.dot(
            weights, jnp.concatenate([v_all[at], ones], axis=1), preferred_element_type=F32
        )
        weighted = jnp.where(low_half, sums[:tile, :LANES], sums[tile:, :LANES])
        totals = jnp.where(low_half, sums[:tile, LANES:], sums[tile:, LANES:])
        return (weighted / totals).astype(BF16)

    def attend_pair(at):
        k_far(at).wait_recv()
        v_far(at).wait_recv()
        q_col(at).wait_recv()
        att_out[at] = attend(at, own_rows)
        att_col(at).start()
        att_own[at] = attend(at, col_rows)

    grid_cols = hid_in.shape[1]
    for at in range(pairs):
        k_col(at).wait_recv()
        k_far(at).start()
        v_col(at).wait_recv()
        v_far(at).start()
        if at == 0:
            load_hid.wait()
            for line in range(hid_in.shape[0]):
                hid[grid_cols * line : grid_cols * (line + 1), :] = hid_in[line]
        else:
            attend_pair(at - 1)
        if torus and at == 0:
            spread_near(0)
        if torus and at == 1:
            spread_near(1)
        if torus and at == pairs - 1:
            for part in range(2):
                across_x(part, 0, colour + 3).wait_recv()
                across_row(colour + 3, part, 10 + part).start()
                across_x(part, 1, colour + 1).wait_recv()
                across_row(colour + 1, part, 12 + part).start()
                across_z(part, colour + 2).wait_recv()
                across_row(colour + 2, part, 14 + part).start()
        if at == 1:
            load_fw.wait()
            fw_row.wait()
            fw_full[:, 0:half] = fw[0]
            fw_full[:, half:features] = fw[1]
    attend_pair(pairs - 1)

    def project(attended, weights):
        joined = jnp.concatenate([attended[at] for at in range(pairs)], axis=1)
        return lax.dot_general(
            joined, weights[...], (((1,), (1,)), ((), ())), preferred_element_type=F32
        ).astype(BF16)

    load_w.wait()
    w_row.wait()
    p_own[...] = project(att_own, w_own)
    if torus:
        for part in range(2):
            across_row(colour, part, 8 + part).wait()
            across_row(colour + 3, part, 10 + part).wait()
            across_row(colour + 1, part, 12 + part).wait()
            across_row(colour + 2, part, 14 + part).wait()
    else:
        near.wait()
        w_far = remote(w_oth.at[own_half], w_oth.at[own_half], weight, 1, to_row)
        w_far.start()
        w_far.wait()
    for at in range(pairs):
        att_col(at).wait_recv()
    p_oth[...] = project(att_in, w_oth)
    load_mod.wait()

    rows = tile // 3

    @pl.loop(0, 3)
    def _(at):
        part = pl.ds(pl.multiple_of(at * rows, 16), rows)
        projected = p_own[part, :].astype(F32) + p_oth[part, :].astype(F32)
        mixed = hid[part, :].astype(F32) + mod[2:3, :] * projected
        mean = jnp.sum(mixed, axis=-1, keepdims=True) * (1.0 / features)
        centered = mixed - mean
        var = jnp.sum(centered * centered, axis=-1, keepdims=True) * (1.0 / features)
        normed = centered * lax.rsqrt(var + EPS) * (1.0 + mod[1:2, :]) + mod[0:1, :]
        vel_ref[part, :] = lax.dot_general(
            normed.astype(BF16), fw_full[...], (((1,), (1,)), ((), ())),
            preferred_element_type=F32,
        )

    for at in range(pairs):
        for copy in (k_col, v_col, q_col, k_far, v_far, att_col):
            copy(at).wait_send()
    if torus:
        for part in range(2):
            near(part).wait_send()
            across_x(part, 0, colour).wait_send()
            across_x(part, 1, colour).wait_send()
            across_z(part, colour).wait_send()


def on_device(
    torus,
    image_qkv, text_kv, gain_query, gain_key, gain_text, out_weight, final_weight,
    hidden, modulation, latent, step_index, step_count,
):
    tile_rows, tile_cols, _, heads_width = image_qkv.shape
    tile = tile_rows * tile_cols
    words, _, width = text_kv.shape
    half = out_weight.shape[1]
    features = hidden.shape[2]
    patch_values = final_weight.shape[0]
    keys = 4 * tile + 2 * words
    pairs = width // LANES
    anywhere = pl.BlockSpec(memory_space=pl.ANY)
    vmem = pl.BlockSpec(memory_space=pltpu.VMEM)
    velocity = pl.pallas_call(
        functools.partial(block_kernel, torus),
        out_shape=jax.ShapeDtypeStruct((tile, patch_values), F32),
        in_specs=[anywhere, anywhere, vmem, vmem, vmem, anywhere, anywhere, anywhere, anywhere],
        out_specs=vmem,
        scratch_shapes=[
            pltpu.VMEM((tile, 3, heads_width), BF16),
            pltpu.VMEM((words, 2, width), BF16),
            pltpu.VMEM((tile_rows, tile_cols, features), BF16),
            pltpu.VMEM((tile, features), BF16),
            pltpu.VMEM((3, features), F32),
            pltpu.VMEM((2, patch_values, half), BF16),
            pltpu.VMEM((patch_values, features), BF16),
            pltpu.VMEM((8, LANES), F32),
            pltpu.VMEM((2 * LANES, LANES), BF16),
            pltpu.VMEM((pairs, tile, LANES), BF16),
            pltpu.VMEM((pairs, tile, LANES), BF16),
            pltpu.VMEM((pairs, tile, LANES), BF16),
            pltpu.VMEM((pairs, 2 * tile, LANES), BF16),
            pltpu.VMEM((pairs, keys, LANES), BF16),
            pltpu.VMEM((pairs, keys, LANES), BF16),
            pltpu.VMEM((features, width), BF16),
            pltpu.VMEM((features, width), BF16),
            pltpu.VMEM((pairs, tile, LANES), BF16),
            pltpu.VMEM((pairs, tile, LANES), BF16),
            pltpu.VMEM((pairs, tile, LANES), BF16),
            pltpu.VMEM((tile, features), BF16),
            pltpu.VMEM((tile, features), BF16),
            pltpu.SemaphoreType.DMA((6,)),
            pltpu.SemaphoreType.DMA((6,)),
            pltpu.SemaphoreType.DMA((6,)),
            pltpu.SemaphoreType.DMA((6 * pairs,)),
            pltpu.SemaphoreType.DMA((6 * pairs,)),
            pltpu.SemaphoreType.DMA((16,)),
            pltpu.SemaphoreType.DMA((16,)),
        ],
        compiler_params=pltpu.CompilerParams(collective_id=0, has_side_effects=True),
        name="attention_block",
    )(
        image_qkv.reshape(tile, 3, heads_width), text_kv,
        gain_query.reshape(1, HEAD), gain_key.reshape(1, HEAD), gain_text.reshape(1, HEAD),
        out_weight.T, final_weight, hidden, modulation,
    )
    velocity = (
        velocity.reshape(tile_rows, tile_cols, PATCH, PATCH, CH)
        .transpose(0, 2, 1, 3, 4)
        .reshape(tile_rows * PATCH, tile_cols * PATCH * CH)
    )
    euler_step = noise_level(step_index[0] + step_count[0]) - noise_level(step_index[0])
    return (velocity, latent + euler_step * velocity)


def solution(mesh):
    placed = (
        P(("req", "row"), "col", None, None),
        P(("req", "row"), None, "col"),
        P(),
        P(),
        P(),
        P("col", "row"),
        P(None, "row"),
        P(("req", "row"), "col", None),
        P("req", None),
        P(("req", "row"), "col"),
        P("req"),
        P("req"),
    )
    torus = TORUS if mesh.shape["req"] == TORUS[0] * TORUS[1] * TORUS[2] else None
    return jax.shard_map(
        functools.partial(on_device, torus),
        mesh=mesh,
        in_specs=placed,
        out_specs=(P(("req", "row"), "col"), P(("req", "row"), "col")),
        check_vma=False,
    )
```

```python
import functools

import jax
import jax.numpy as jnp
from jax import lax
from jax.experimental import pallas as pl
from jax.experimental.pallas import tpu as pltpu
from jax.sharding import PartitionSpec as P

HEAD = 64
CH = 16
PATCH = 2
STEPS = 28
SHIFT_FACTOR = 3.0
EPS = 1e-06
LANES = 128
TORUS = (4, 4, 8)
MESH = pl.DeviceIdType.MESH
F32, BF16 = jnp.float32, jnp.bfloat16


def noise_level(step_number):
    fraction = 1.0 - jnp.full((1, 1), step_number, jnp.int32).astype(F32) / STEPS
    return SHIFT_FACTOR * fraction / (1.0 + (SHIFT_FACTOR - 1.0) * fraction)


def block_kernel(
    torus,
    qkv_hbm, text_hbm, gq_hbm, gk_hbm, gt_hbm, wt_hbm, fw_hbm, hid_hbm, mod_hbm,
    lat_hbm, index_ref, count_ref,
    out_ref,
    qkv, text, hid_in, hid, mod, fw, fw_full, gain_in, gains, block, lat, patch, pixels,
    v_out, k_out, q_out, q_all, k_all, v_all, w_own, w_oth,
    att_out, att_in, att_own, p_own, p_oth, base,
    load_sem, send_sem, recv_sem, pair_send, pair_recv, w_send, w_recv,
):
    row, col = lax.axis_index("row"), lax.axis_index("col")
    to_row, to_col = {"row": 1 - row}, {"col": 1 - col}
    tile = qkv.shape[0]
    words = text.shape[0]
    pairs, keys, _ = k_all.shape
    width = pairs * LANES
    half = wt_hbm.shape[0]
    features = w_own.shape[0]

    def load(source, target, at):
        return pltpu.make_async_copy(source, target, load_sem.at[at])

    def remote(source, target, sems, at, device):
        return pltpu.make_async_remote_copy(
            src_ref=source, dst_ref=target, send_sem=sems[0].at[at], recv_sem=sems[1].at[at],
            device_id=device, device_id_type=MESH,
        )

    plain, paired, weight = (send_sem, recv_sem), (pair_send, pair_recv), (w_send, w_recv)

    own_half = pl.ds(pl.multiple_of(row * half, 64), half)
    load_qkv = load(qkv_hbm, qkv, 0)
    load_text = load(text_hbm, text, 1)
    load_w = load(wt_hbm, w_own.at[own_half], 2)
    load_fw = load(fw_hbm, fw.at[row], 3)
    load_hid = load(hid_hbm, hid_in, 4)
    load_mod = load(mod_hbm, mod, 5)
    load_lat = load(lat_hbm, lat, 6)
    load_gains = [load(ref, gain_in.at[at], 7 + at) for at, ref in enumerate((gq_hbm, gk_hbm, gt_hbm))]
    load_qkv.start()
    for copy in load_gains:
        copy.start()

    partners = [to_row, to_col]
    if torus:
        size_x, size_y, size_z = torus
        req = lax.axis_index("req")
        at_z = req % size_z
        at_y = (req // size_z) % size_y
        at_x = req // (size_z * size_y)

        def chip(x, y, z):
            return ((x % size_x) * size_y + y % size_y) * size_z + z % size_z

        to_y = {"req": chip(at_x, at_y + size_y + 2 * col - 1, at_z), "col": 1 - col}
        to_x = [{"req": chip(at_x + step, at_y, at_z)} for step in (1, size_x - 1)]
        partners += [to_y, *to_x]

    barrier = pltpu.get_barrier_semaphore()
    for partner in partners:
        pl.semaphore_signal(barrier, inc=1, device_id=partner, device_id_type=MESH)

    down = lax.broadcasted_iota(jnp.int32, (2 * LANES, LANES), 0) // HEAD
    across = lax.broadcasted_iota(jnp.int32, (2 * LANES, LANES), 1) // HEAD
    block[...] = jnp.where(down % 2 == across, 1.0 / HEAD, 0.0).astype(BF16)

    for at, copy in enumerate(load_gains):
        copy.wait()
        gains[at : at + 1, 0:HEAD] = gain_in[at]
        gains[at : at + 1, HEAD:LANES] = gain_in[at]

    pl.semaphore_wait(barrier, len(partners))

    if torus:
        quarter = half // 4
        first = quarter // 32 * 16 + 16
        parts = ((0, first), (first, quarter - first))

        def piece(which, part, base):
            start, count = parts[part]
            offset = base + (which % 4) * quarter + start
            return pl.ds(pl.multiple_of(offset, 16), count)

        def near(side, part):
            which = at_x + 2 * side
            return remote(
                wt_hbm.at[piece(which, part, 0)],
                w_oth.at[piece(which, part, row * half)], weight, 2 * side + part, to_y,
            )

        def spread(which, part, at, device):
            rows = piece(which, part, row * half)
            return remote(w_oth.at[rows], w_oth.at[rows], weight, at, device)

        def across_x(part, side, which):
            return spread(which, part, 4 + 2 * side + part, to_x[side])

        def across_row(part, away):
            return spread(at_x + away, part, 8 + 2 * away + part, to_row)

        for side in range(2):
            for part in range(2):
                near(side, part).start()
    else:
        near = remote(wt_hbm, w_oth.at[own_half], weight, 0, to_col)
    w_row = remote(wt_hbm, w_own.at[own_half], plain, 0, to_row)
    fw_row = remote(fw_hbm, fw.at[row], plain, 1, to_row)

    def head_norm(values, gain):
        count = values.shape[0]
        pieces = [values[:, LANES * at : LANES * (at + 1)] for at in range(pairs)]
        stacked = jnp.concatenate(pieces, axis=0).astype(F32)
        square = stacked * stacked
        high = square.astype(BF16)
        low = (square - high.astype(F32)).astype(BF16)
        mean = jnp.dot(
            jnp.concatenate([high, low], axis=1), block[...], preferred_element_type=F32
        )
        normed = (stacked * lax.rsqrt(mean + EPS) * gain).astype(BF16)
        return normed.reshape(pairs, count, LANES)

    def split(values):
        return [values[:, LANES * at : LANES * (at + 1)] for at in range(pairs)]

    mine = pl.ds(pl.multiple_of(col * width, LANES), width)
    other = pl.ds(pl.multiple_of((1 - col) * width, LANES), width)
    own_rows, col_rows = pl.ds(0, tile), pl.ds(tile, tile)
    row_rows, far_rows = pl.ds(2 * tile, tile), pl.ds(3 * tile, tile)
    own_text, row_text = pl.ds(4 * tile, words), pl.ds(4 * tile + words, words)

    def k_col(at):
        return remote(k_out.at[at], k_all.at[at, col_rows], paired, at, to_col)

    def v_col(at):
        return remote(v_out.at[at], v_all.at[at, col_rows], paired, pairs + at, to_col)

    def q_col(at):
        return remote(q_out.at[at], q_all.at[at, own_rows], paired, 2 * pairs + at, to_col)

    def k_far(at):
        return remote(
            k_all.at[at, col_rows], k_all.at[at, far_rows], paired, 3 * pairs + at, to_row
        )

    def v_far(at):
        return remote(
            v_all.at[at, col_rows], v_all.at[at, far_rows], paired, 4 * pairs + at, to_row
        )

    def att_col(at):
        return remote(att_out.at[at], att_in.at[at], paired, 5 * pairs + at, to_col)

    load_qkv.wait()
    for copy in (load_text, load_w, load_fw, load_hid, load_mod, load_lat):
        copy.start()
    for at, part in enumerate(split(qkv[:, 2, other])):
        v_out[at] = part
    v_col(0).start()
    v_col(1).start()
    k_out[...] = head_norm(qkv[:, 1, other], gains[1:2])
    k_col(0).start()
    q_out[...] = head_norm(qkv[:, 0, other], gains[0:1] * 0.125)
    q_col(0).start()
    k_col(1).start()
    q_col(1).start()
    for at in range(2, pairs):
        k_col(at).start()
        v_col(at).start()
        q_col(at).start()

    for at, part in enumerate(split(qkv[:, 2, mine])):
        v_all[at, own_rows, :] = part
    v_row = remote(v_all.at[:, own_rows], v_all.at[:, row_rows], plain, 2, to_row)
    v_row.start()
    k_all[:, own_rows, :] = head_norm(qkv[:, 1, mine], gains[1:2])
    k_row = remote(k_all.at[:, own_rows], k_all.at[:, row_rows], plain, 3, to_row)
    k_row.start()
    load_text.wait()
    for at, part in enumerate(split(text[:, 1, :])):
        v_all[at, own_text, :] = part
    vt_row = remote(v_all.at[:, own_text], v_all.at[:, row_text], plain, 4, to_row)
    vt_row.start()
    k_all[:, own_text, :] = head_norm(text[:, 0, :], gains[2:3])
    kt_row = remote(k_all.at[:, own_text], k_all.at[:, row_text], plain, 5, to_row)
    kt_row.start()
    w_row.start()
    fw_row.start()
    if not torus:
        near.start()
    q_all[:, col_rows, :] = head_norm(qkv[:, 0, mine], gains[0:1] * 0.125)

    def spread_near(part):
        near(0, part).wait_recv()
        across_x(part, 0, at_x).start()
        across_x(part, 1, at_x).start()
        across_row(part, 0).start()

    def pass_x(part):
        across_x(part, 0, at_x + 3).wait_recv()
        across_row(part, 3).start()
        across_x(part, 1, at_x + 1).wait_recv()
        across_row(part, 1).start()

    def pass_near(part):
        near(1, part).wait_recv()
        across_row(part, 2).start()

    v_row.wait()
    k_row.wait()
    vt_row.wait()
    kt_row.wait()

    low_half = lax.broadcasted_iota(jnp.int32, (tile, LANES), 1) < HEAD
    ones = jnp.ones((keys, LANES), BF16)

    def attend(at, rows):
        pair = q_all[at, rows, :].astype(F32)
        both = jnp.concatenate(
            [jnp.where(low_half, pair, 0.0), jnp.where(low_half, 0.0, pair)], axis=0
        ).astype(BF16)
        scores = lax.dot_general(
            both, k_all[at], (((1,), (1,)), ((), ())), preferred_element_type=F32
        )
        weights = jnp.exp(scores).astype(BF16)
        sums = jnp.dot(
            weights, jnp.concatenate([v_all[at], ones], axis=1), preferred_element_type=F32
        )
        weighted = jnp.where(low_half, sums[:tile, :LANES], sums[tile:, :LANES])
        totals = jnp.where(low_half, sums[:tile, LANES:], sums[tile:, LANES:])
        return (weighted / totals).astype(BF16)

    def attend_pair(at):
        k_far(at).wait_recv()
        v_far(at).wait_recv()
        q_col(at).wait_recv()
        att_out[at] = attend(at, own_rows)
        att_col(at).start()
        att_own[at] = attend(at, col_rows)

    grid_cols = hid_in.shape[1]
    for at in range(pairs):
        k_col(at).wait_recv()
        k_far(at).start()
        v_col(at).wait_recv()
        v_far(at).start()
        if torus and at == 1:
            spread_near(0)
        if at > 0:
            attend_pair(at - 1)
        if at == 0:
            load_hid.wait()
            for line in range(hid_in.shape[0]):
                hid[grid_cols * line : grid_cols * (line + 1), :] = hid_in[line]
            load_fw.wait()
            fw_row.wait()
            fw_full[:, 0:half] = fw[0]
            fw_full[:, half:features] = fw[1]
        if torus and at == 2:
            spread_near(1)
        if torus and at == 3:
            pass_x(0)
        if torus and at == 4:
            pass_near(0)
    attend_pair(pairs - 1)
    if torus:
        pass_x(1)

    def project(attended, weights):
        joined = jnp.concatenate([attended[at] for at in range(pairs)], axis=1)
        return lax.dot_general(
            joined, weights[...], (((1,), (1,)), ((), ())), preferred_element_type=F32
        ).astype(BF16)

    rows = tile // 3
    load_w.wait()
    w_row.wait()
    load_mod.wait()
    p_own[...] = project(att_own, w_own)

    @pl.loop(0, 3)
    def _(at):
        part = pl.ds(pl.multiple_of(at * rows, 16), rows)
        base[part, :] = hid[part, :].astype(F32) + mod[2:3, :] * p_own[part, :].astype(F32)

    if torus:
        pass_near(1)
        for part in range(2):
            for away in range(4):
                across_row(part, away).wait()
    else:
        near.wait()
        w_far = remote(w_oth.at[own_half], w_oth.at[own_half], weight, 1, to_row)
        w_far.start()
        w_far.wait()
    for at in range(pairs):
        att_col(at).wait_recv()
    p_oth[...] = project(att_in, w_oth)

    @pl.loop(0, 3)
    def _(at):
        part = pl.ds(pl.multiple_of(at * rows, 16), rows)
        mixed = base[part, :] + mod[2:3, :] * p_oth[part, :].astype(F32)
        mean = jnp.sum(mixed, axis=-1, keepdims=True) * (1.0 / features)
        centered = mixed - mean
        var = jnp.sum(centered * centered, axis=-1, keepdims=True) * (1.0 / features)
        normed = centered * lax.rsqrt(var + EPS) * (1.0 + mod[1:2, :]) + mod[0:1, :]
        patch[part, 0:HEAD] = lax.dot_general(
            normed.astype(BF16), fw_full[...], (((1,), (1,)), ((), ())),
            preferred_element_type=F32,
        )

    load_lat.wait()
    span = PATCH * CH
    side = tile // grid_cols
    lane = lax.broadcasted_iota(jnp.int32, (side, LANES), 1) // span
    euler = noise_level(index_ref[0] + count_ref[0]) - noise_level(index_ref[0])
    step = LANES // span
    for first_col in range(0, grid_cols, step):
        columns = [
            patch[pl.ds(first_col + at, side, stride=grid_cols), :] for at in range(step)
        ]
        lanes = slice(first_col * span, (first_col + step) * span)
        for line in range(PATCH):
            merged = jnp.zeros((side, LANES), F32)
            for at, values in enumerate(columns):
                moved = pltpu.roll(values, (at - line) % step * span, 1)
                merged = jnp.where(lane == at, moved, merged)
            pixels[first_col // step, pl.ds(line, side, stride=PATCH), :] = merged
        velocity = pixels[first_col // step]
        out_ref[0, :, lanes] = velocity
        out_ref[1, :, lanes] = lat[:, lanes] + euler * velocity

    for at in range(pairs):
        for copy in (k_col, v_col, q_col, k_far, v_far, att_col):
            copy(at).wait_send()
    if torus:
        for part in range(2):
            near(0, part).wait_send()
            near(1, part).wait_send()
            across_x(part, 0, at_x).wait_send()
            across_x(part, 1, at_x).wait_send()


def on_device(
    torus,
    image_qkv, text_kv, gain_query, gain_key, gain_text, out_weight, final_weight,
    hidden, modulation, latent, step_index, step_count,
):
    tile_rows, tile_cols, _, heads_width = image_qkv.shape
    tile = tile_rows * tile_cols
    words, _, width = text_kv.shape
    half = out_weight.shape[1]
    features = hidden.shape[2]
    patch_values = final_weight.shape[0]
    keys = 4 * tile + 2 * words
    pairs = width // LANES
    anywhere = pl.BlockSpec(memory_space=pltpu.HBM)
    vmem = pl.BlockSpec(memory_space=pltpu.VMEM)
    both = pl.pallas_call(
        functools.partial(block_kernel, torus),
        out_shape=jax.ShapeDtypeStruct((2, *latent.shape), F32),
        in_specs=[anywhere] * 10 + [pl.BlockSpec(memory_space=pltpu.SMEM)] * 2,
        out_specs=vmem,
        scratch_shapes=[
            pltpu.VMEM((tile, 3, heads_width), BF16),
            pltpu.VMEM((words, 2, width), BF16),
            pltpu.VMEM((tile_rows, tile_cols, features), BF16),
            pltpu.VMEM((tile, features), BF16),
            pltpu.VMEM((3, features), F32),
            pltpu.VMEM((2, patch_values, half), BF16),
            pltpu.VMEM((patch_values, features), BF16),
            pltpu.VMEM((3, 1, HEAD), F32),
            pltpu.VMEM((8, LANES), F32),
            pltpu.VMEM((2 * LANES, LANES), BF16),
            pltpu.VMEM(latent.shape, F32),
            pltpu.VMEM((tile, LANES), F32),
            pltpu.VMEM((latent.shape[1] // LANES, latent.shape[0], LANES), F32),
            pltpu.VMEM((pairs, tile, LANES), BF16),
            pltpu.VMEM((pairs, tile, LANES), BF16),
            pltpu.VMEM((pairs, tile, LANES), BF16),
            pltpu.VMEM((pairs, 2 * tile, LANES), BF16),
            pltpu.VMEM((pairs, keys, LANES), BF16),
            pltpu.VMEM((pairs, keys, LANES), BF16),
            pltpu.VMEM((features, width), BF16),
            pltpu.VMEM((features, width), BF16),
            pltpu.VMEM((pairs, tile, LANES), BF16),
            pltpu.VMEM((pairs, tile, LANES), BF16),
            pltpu.VMEM((pairs, tile, LANES), BF16),
            pltpu.VMEM((tile, features), BF16),
            pltpu.VMEM((tile, features), BF16),
            pltpu.VMEM((tile, features), F32),
            pltpu.SemaphoreType.DMA((10,)),
            pltpu.SemaphoreType.DMA((6,)),
            pltpu.SemaphoreType.DMA((6,)),
            pltpu.SemaphoreType.DMA((6 * pairs,)),
            pltpu.SemaphoreType.DMA((6 * pairs,)),
            pltpu.SemaphoreType.DMA((16,)),
            pltpu.SemaphoreType.DMA((16,)),
        ],
        compiler_params=pltpu.CompilerParams(
            collective_id=0, has_side_effects=True, vmem_limit_bytes=40 * 1024 * 1024
        ),
        name="attention_block",
    )(
        *(
            pltpu.with_memory_space_constraint(operand, pltpu.HBM)
            for operand in (
                image_qkv.reshape(tile, 3, heads_width), text_kv,
                gain_query.reshape(1, HEAD), gain_key.reshape(1, HEAD),
                gain_text.reshape(1, HEAD), out_weight.T, final_weight, hidden, modulation,
                latent,
            )
        ),
        step_index, step_count,
    )
    return (both[0], both[1])


def solution(mesh):
    placed = (
        P(("req", "row"), "col", None, None),
        P(("req", "row"), None, "col"),
        P(),
        P(),
        P(),
        P("col", "row"),
        P(None, "row"),
        P(("req", "row"), "col", None),
        P("req", None),
        P(("req", "row"), "col"),
        P("req"),
        P("req"),
    )
    torus = TORUS if mesh.shape["req"] == TORUS[0] * TORUS[1] * TORUS[2] else None
    return jax.shard_map(
        functools.partial(on_device, torus),
        mesh=mesh,
        in_specs=placed,
        out_specs=(P(("req", "row"), "col"), P(("req", "row"), "col")),
        check_vma=False,
    )
```

```python
import functools

import jax
import jax.numpy as jnp
from jax import lax
from jax.experimental import pallas as pl
from jax.experimental.pallas import tpu as pltpu
from jax.sharding import PartitionSpec as P

HEAD = 64
CH = 16
PATCH = 2
STEPS = 28
SHIFT_FACTOR = 3.0
EPS = 1e-06
LANES = 128
TORUS = (4, 4, 8)
MESH = pl.DeviceIdType.MESH
F32, BF16 = jnp.float32, jnp.bfloat16


def noise_level(step_number):
    fraction = 1.0 - jnp.full((1, 1), step_number, jnp.int32).astype(F32) / STEPS
    return SHIFT_FACTOR * fraction / (1.0 + (SHIFT_FACTOR - 1.0) * fraction)


def block_kernel(
    torus,
    qkv_hbm, text_hbm, gq_hbm, gk_hbm, gt_hbm, wt_hbm, fw_hbm, hid_hbm, mod_hbm,
    lat_hbm, index_ref, count_ref,
    out_ref,
    qkv, text, hid_in, hid, mod, fw, fw_full, gain_in, gains, block, lat, patch, pixels,
    v_out, k_out, q_out, q_all, k_all, v_all, w_own, w_oth,
    att_out, att_in, att_own, p_oth, base,
    load_sem, send_sem, recv_sem, pair_send, pair_recv, w_send, w_recv,
):
    row, col = lax.axis_index("row"), lax.axis_index("col")
    to_row, to_col = {"row": 1 - row}, {"col": 1 - col}
    tile = qkv.shape[0]
    words = text.shape[0]
    pairs, keys, _ = k_all.shape
    width = pairs * LANES
    half = wt_hbm.shape[0]
    features = w_own.shape[0]

    def load(source, target, at):
        return pltpu.make_async_copy(source, target, load_sem.at[at])

    def remote(source, target, sems, at, device):
        return pltpu.make_async_remote_copy(
            src_ref=source, dst_ref=target, send_sem=sems[0].at[at], recv_sem=sems[1].at[at],
            device_id=device, device_id_type=MESH,
        )

    plain, paired, weight = (send_sem, recv_sem), (pair_send, pair_recv), (w_send, w_recv)

    own_half = pl.ds(pl.multiple_of(row * half, 64), half)
    load_qkv = load(qkv_hbm, qkv, 0)
    load_text = load(text_hbm, text, 1)
    load_w = load(wt_hbm, w_own.at[own_half], 2)
    load_fw = load(fw_hbm, fw.at[row], 3)
    load_hid = load(hid_hbm, hid_in, 4)
    load_mod = load(mod_hbm, mod, 5)
    load_lat = load(lat_hbm, lat, 6)
    load_gains = [load(ref, gain_in.at[at], 7 + at) for at, ref in enumerate((gq_hbm, gk_hbm, gt_hbm))]
    load_qkv.start()
    for copy in load_gains:
        copy.start()

    partners = [to_row, to_col]
    if torus:
        size_x, size_y, size_z = torus
        req = lax.axis_index("req")
        at_z = req % size_z
        at_y = (req // size_z) % size_y
        at_x = req // (size_z * size_y)

        def chip(x, y, z):
            return ((x % size_x) * size_y + y % size_y) * size_z + z % size_z

        to_y = {"req": chip(at_x, at_y + size_y + 2 * col - 1, at_z), "col": 1 - col}
        to_x = [{"req": chip(at_x + step, at_y, at_z)} for step in (1, size_x - 1)]
        partners += [to_y, *to_x]

    barrier = pltpu.get_barrier_semaphore()
    for partner in partners:
        pl.semaphore_signal(barrier, inc=1, device_id=partner, device_id_type=MESH)

    down = lax.broadcasted_iota(jnp.int32, (2 * LANES, LANES), 0) // HEAD
    across = lax.broadcasted_iota(jnp.int32, (2 * LANES, LANES), 1) // HEAD
    block[...] = jnp.where(down % 2 == across, 1.0 / HEAD, 0.0).astype(BF16)

    for at, copy in enumerate(load_gains):
        copy.wait()
        gains[at : at + 1, 0:HEAD] = gain_in[at]
        gains[at : at + 1, HEAD:LANES] = gain_in[at]

    pl.semaphore_wait(barrier, len(partners))

    if torus:
        quarter = half // 4
        third = quarter // 48 * 16
        parts = ((0, third), (third, quarter - 2 * third), (quarter - third, third))

        def piece(which, part, base):
            start, count = parts[part]
            offset = base + (which % 4) * quarter + start
            return pl.ds(pl.multiple_of(offset, 16), count)

        def near(side, part):
            which = at_x + 2 * side
            return remote(
                wt_hbm.at[piece(which, part, 0)],
                w_oth.at[piece(which, part, row * half)], weight, 2 * side + part, to_y,
            )

        def spread(which, part, at, device):
            rows = piece(which, part, row * half)
            return remote(w_oth.at[rows], w_oth.at[rows], weight, at, device)

        def across_x(part, side, which):
            return spread(which, part, 5 + 3 * side + part, to_x[side])

        def across_two(which):
            return spread(which, 0, 11, to_x[0])

        def across_row(part, away):
            return spread(at_x + away, part, 12 + 3 * away + part, to_row)

        for part in range(3):
            near(0, part).start()
        near(1, 1).start()
        near(1, 2).start()
    else:
        near = remote(wt_hbm, w_oth.at[own_half], weight, 0, to_col)
    w_row = remote(wt_hbm, w_own.at[own_half], plain, 0, to_row)
    fw_row = remote(fw_hbm, fw.at[row], plain, 1, to_row)
    w_row.start()
    fw_row.start()

    def head_norm(values, gain):
        count = values.shape[0]
        pieces = [values[:, LANES * at : LANES * (at + 1)] for at in range(pairs)]
        stacked = jnp.concatenate(pieces, axis=0).astype(F32)
        square = stacked * stacked
        high = square.astype(BF16)
        low = (square - high.astype(F32)).astype(BF16)
        mean = jnp.dot(
            jnp.concatenate([high, low], axis=1), block[...], preferred_element_type=F32
        )
        normed = (stacked * lax.rsqrt(mean + EPS) * gain).astype(BF16)
        return normed.reshape(pairs, count, LANES)

    def split(values):
        return [values[:, LANES * at : LANES * (at + 1)] for at in range(pairs)]

    mine = pl.ds(pl.multiple_of(col * width, LANES), width)
    other = pl.ds(pl.multiple_of((1 - col) * width, LANES), width)
    own_rows, col_rows = pl.ds(0, tile), pl.ds(tile, tile)
    row_rows, far_rows = pl.ds(2 * tile, tile), pl.ds(3 * tile, tile)
    own_text, row_text = pl.ds(4 * tile, words), pl.ds(4 * tile + words, words)

    def k_col(at):
        return remote(k_out.at[at], k_all.at[at, col_rows], paired, at, to_col)

    def v_col(at):
        return remote(v_out.at[at], v_all.at[at, col_rows], paired, pairs + at, to_col)

    def q_col(at):
        return remote(q_out.at[at], q_all.at[at, own_rows], paired, 2 * pairs + at, to_col)

    def k_far(at):
        return remote(
            k_all.at[at, col_rows], k_all.at[at, far_rows], paired, 3 * pairs + at, to_row
        )

    def v_far(at):
        return remote(
            v_all.at[at, col_rows], v_all.at[at, far_rows], paired, 4 * pairs + at, to_row
        )

    def att_col(at):
        return remote(att_out.at[at], att_in.at[at], paired, 5 * pairs + at, to_col)

    load_qkv.wait()
    for copy in (load_text, load_w, load_fw, load_hid, load_mod, load_lat):
        copy.start()
    for at, part in enumerate(split(qkv[:, 2, other])):
        v_out[at] = part
    v_col(0).start()
    v_col(1).start()
    k_out[...] = head_norm(qkv[:, 1, other], gains[1:2])
    k_col(0).start()
    q_out[...] = head_norm(qkv[:, 0, other], gains[0:1] * 0.125)
    q_col(0).start()
    k_col(1).start()
    q_col(1).start()
    for at in range(2, pairs):
        k_col(at).start()
        v_col(at).start()
        q_col(at).start()

    for at, part in enumerate(split(qkv[:, 2, mine])):
        v_all[at, own_rows, :] = part
    v_row = remote(v_all.at[:, own_rows], v_all.at[:, row_rows], plain, 2, to_row)
    v_row.start()
    k_all[:, own_rows, :] = head_norm(qkv[:, 1, mine], gains[1:2])
    k_row = remote(k_all.at[:, own_rows], k_all.at[:, row_rows], plain, 3, to_row)
    k_row.start()
    load_text.wait()
    for at, part in enumerate(split(text[:, 1, :])):
        v_all[at, own_text, :] = part
    vt_row = remote(v_all.at[:, own_text], v_all.at[:, row_text], plain, 4, to_row)
    vt_row.start()
    k_all[:, own_text, :] = head_norm(text[:, 0, :], gains[2:3])
    kt_row = remote(k_all.at[:, own_text], k_all.at[:, row_text], plain, 5, to_row)
    kt_row.start()
    if not torus:
        near.start()
    q_all[:, col_rows, :] = head_norm(qkv[:, 0, mine], gains[0:1] * 0.125)

    def spread_near(part):
        near(0, part).wait_recv()
        across_x(part, 0, at_x).start()
        across_x(part, 1, at_x).start()
        across_row(part, 0).start()

    def pass_x(part):
        across_x(part, 0, at_x + 3).wait_recv()
        if part == 0:
            across_two(at_x + 3).start()
        across_row(part, 3).start()
        across_x(part, 1, at_x + 1).wait_recv()
        across_row(part, 1).start()

    def pass_near(part):
        near(1, part).wait_recv()
        across_row(part, 2).start()

    v_row.wait()
    k_row.wait()
    vt_row.wait()
    kt_row.wait()

    low_half = lax.broadcasted_iota(jnp.int32, (tile, LANES), 1) < HEAD
    ones = jnp.ones((keys, LANES), BF16)

    def attend(at, rows):
        pair = q_all[at, rows, :].astype(F32)
        both = jnp.concatenate(
            [jnp.where(low_half, pair, 0.0), jnp.where(low_half, 0.0, pair)], axis=0
        ).astype(BF16)
        scores = lax.dot_general(
            both, k_all[at], (((1,), (1,)), ((), ())), preferred_element_type=F32
        )
        weights = jnp.exp(scores).astype(BF16)
        sums = jnp.dot(
            weights, jnp.concatenate([v_all[at], ones], axis=1), preferred_element_type=F32
        )
        weighted = jnp.where(low_half, sums[:tile, :LANES], sums[tile:, :LANES])
        totals = jnp.where(low_half, sums[:tile, LANES:], sums[tile:, LANES:])
        return (weighted / totals).astype(BF16)

    def attend_pair(at):
        k_far(at).wait_recv()
        v_far(at).wait_recv()
        q_col(at).wait_recv()
        att_out[at] = attend(at, own_rows)
        att_col(at).start()
        att_own[at] = attend(at, col_rows)

    def project(attended, weights, first, last):
        joined = jnp.concatenate([attended[at] for at in range(first, last)], axis=1)
        return lax.dot_general(
            joined, weights[:, LANES * first : LANES * last], (((1,), (1,)), ((), ())),
            preferred_element_type=F32,
        )

    grid_cols = hid_in.shape[1]
    for at in range(pairs):
        k_col(at).wait_recv()
        k_far(at).start()
        v_col(at).wait_recv()
        v_far(at).start()
        if torus and at < 2:
            spread_near(at)
        if torus and at == 3:
            pass_x(0)
        if at > 0:
            attend_pair(at - 1)
        if at == 0:
            load_hid.wait()
            for line in range(hid_in.shape[0]):
                hid[grid_cols * line : grid_cols * (line + 1), :] = hid_in[line]
            load_fw.wait()
            fw_row.wait()
            fw_full[:, 0:half] = fw[0]
            fw_full[:, half:features] = fw[1]
        if torus and at == 2:
            spread_near(2)
        if torus and at == 3:
            pass_x(1)
        if torus and at == 4:
            pass_near(1)
        if at == 3:
            load_w.wait()
            w_row.wait()
            base[...] = project(att_own, w_own, 0, 2)
    attend_pair(pairs - 1)
    if torus:
        pass_x(2)
        pass_near(2)

    rows = tile // 3
    load_mod.wait()
    base[...] += project(att_own, w_own, 2, pairs)

    @pl.loop(0, 3)
    def _(at):
        part = pl.ds(pl.multiple_of(at * rows, 16), rows)
        product = base[part, :].astype(BF16).astype(F32)
        base[part, :] = hid[part, :].astype(F32) + mod[2:3, :] * product

    if torus:
        across_two(at_x + 2).wait_recv()
        across_row(0, 2).start()
        for part in range(3):
            for away in range(4):
                across_row(part, away).wait()
    else:
        near.wait()
        w_far = remote(w_oth.at[own_half], w_oth.at[own_half], weight, 1, to_row)
        w_far.start()
        w_far.wait()
    for at in range(pairs):
        att_col(at).wait_recv()
    p_oth[...] = project(att_in, w_oth, 0, pairs).astype(BF16)

    @pl.loop(0, 3)
    def _(at):
        part = pl.ds(pl.multiple_of(at * rows, 16), rows)
        mixed = base[part, :] + mod[2:3, :] * p_oth[part, :].astype(F32)
        mean = jnp.sum(mixed, axis=-1, keepdims=True) * (1.0 / features)
        centered = mixed - mean
        var = jnp.sum(centered * centered, axis=-1, keepdims=True) * (1.0 / features)
        normed = centered * lax.rsqrt(var + EPS) * (1.0 + mod[1:2, :]) + mod[0:1, :]
        p_oth[part, :] = normed.astype(BF16)

    patch[:, 0:HEAD] = lax.dot_general(
        p_oth[...], fw_full[...], (((1,), (1,)), ((), ())), preferred_element_type=F32
    )

    load_lat.wait()
    span = PATCH * CH
    side = tile // grid_cols
    lane = lax.broadcasted_iota(jnp.int32, (side, LANES), 1) // span
    euler = noise_level(index_ref[0] + count_ref[0]) - noise_level(index_ref[0])
    step = LANES // span
    for first_col in range(0, grid_cols, step):
        columns = [
            patch[pl.ds(first_col + at, side, stride=grid_cols), :] for at in range(step)
        ]
        lanes = slice(first_col * span, (first_col + step) * span)
        for line in range(PATCH):
            merged = jnp.zeros((side, LANES), F32)
            for at, values in enumerate(columns):
                moved = pltpu.roll(values, (at - line) % step * span, 1)
                merged = jnp.where(lane == at, moved, merged)
            pixels[first_col // step, pl.ds(line, side, stride=PATCH), :] = merged
        velocity = pixels[first_col // step]
        out_ref[0, :, lanes] = velocity
        out_ref[1, :, lanes] = lat[:, lanes] + euler * velocity

    for at in range(pairs):
        for copy in (k_col, v_col, q_col, k_far, v_far, att_col):
            copy(at).wait_send()
    if torus:
        across_two(at_x + 3).wait_send()
        near(1, 1).wait_send()
        near(1, 2).wait_send()
        for part in range(3):
            near(0, part).wait_send()
            across_x(part, 0, at_x).wait_send()
            across_x(part, 1, at_x).wait_send()


def on_device(
    torus,
    image_qkv, text_kv, gain_query, gain_key, gain_text, out_weight, final_weight,
    hidden, modulation, latent, step_index, step_count,
):
    tile_rows, tile_cols, _, heads_width = image_qkv.shape
    tile = tile_rows * tile_cols
    words, _, width = text_kv.shape
    half = out_weight.shape[1]
    features = hidden.shape[2]
    patch_values = final_weight.shape[0]
    keys = 4 * tile + 2 * words
    pairs = width // LANES
    anywhere = pl.BlockSpec(memory_space=pltpu.HBM)
    vmem = pl.BlockSpec(memory_space=pltpu.VMEM)
    both = pl.pallas_call(
        functools.partial(block_kernel, torus),
        out_shape=jax.ShapeDtypeStruct((2, *latent.shape), F32),
        in_specs=[anywhere] * 10 + [pl.BlockSpec(memory_space=pltpu.SMEM)] * 2,
        out_specs=vmem,
        scratch_shapes=[
            pltpu.VMEM((tile, 3, heads_width), BF16),
            pltpu.VMEM((words, 2, width), BF16),
            pltpu.VMEM((tile_rows, tile_cols, features), BF16),
            pltpu.VMEM((tile, features), BF16),
            pltpu.VMEM((3, features), F32),
            pltpu.VMEM((2, patch_values, half), BF16),
            pltpu.VMEM((patch_values, features), BF16),
            pltpu.VMEM((3, 1, HEAD), F32),
            pltpu.VMEM((8, LANES), F32),
            pltpu.VMEM((2 * LANES, LANES), BF16),
            pltpu.VMEM(latent.shape, F32),
            pltpu.VMEM((tile, LANES), F32),
            pltpu.VMEM((latent.shape[1] // LANES, latent.shape[0], LANES), F32),
            pltpu.VMEM((pairs, tile, LANES), BF16),
            pltpu.VMEM((pairs, tile, LANES), BF16),
            pltpu.VMEM((pairs, tile, LANES), BF16),
            pltpu.VMEM((pairs, 2 * tile, LANES), BF16),
            pltpu.VMEM((pairs, keys, LANES), BF16),
            pltpu.VMEM((pairs, keys, LANES), BF16),
            pltpu.VMEM((features, width), BF16),
            pltpu.VMEM((features, width), BF16),
            pltpu.VMEM((pairs, tile, LANES), BF16),
            pltpu.VMEM((pairs, tile, LANES), BF16),
            pltpu.VMEM((pairs, tile, LANES), BF16),
            pltpu.VMEM((tile, features), BF16),
            pltpu.VMEM((tile, features), F32),
            pltpu.SemaphoreType.DMA((10,)),
            pltpu.SemaphoreType.DMA((6,)),
            pltpu.SemaphoreType.DMA((6,)),
            pltpu.SemaphoreType.DMA((6 * pairs,)),
            pltpu.SemaphoreType.DMA((6 * pairs,)),
            pltpu.SemaphoreType.DMA((24,)),
            pltpu.SemaphoreType.DMA((24,)),
        ],
        compiler_params=pltpu.CompilerParams(
            collective_id=0, has_side_effects=True, vmem_limit_bytes=40 * 1024 * 1024
        ),
        name="attention_block",
    )(
        *(
            pltpu.with_memory_space_constraint(operand, pltpu.HBM)
            for operand in (
                image_qkv.reshape(tile, 3, heads_width), text_kv,
                gain_query.reshape(1, HEAD), gain_key.reshape(1, HEAD),
                gain_text.reshape(1, HEAD), out_weight.T, final_weight, hidden, modulation,
                latent,
            )
        ),
        step_index, step_count,
    )
    return (both[0], both[1])


def solution(mesh):
    placed = (
        P(("req", "row"), "col", None, None),
        P(("req", "row"), None, "col"),
        P(),
        P(),
        P(),
        P("col", "row"),
        P(None, "row"),
        P(("req", "row"), "col", None),
        P("req", None),
        P(("req", "row"), "col"),
        P("req"),
        P("req"),
    )
    torus = TORUS if mesh.shape["req"] == TORUS[0] * TORUS[1] * TORUS[2] else None
    return jax.shard_map(
        functools.partial(on_device, torus),
        mesh=mesh,
        in_specs=placed,
        out_specs=(P(("req", "row"), "col"), P(("req", "row"), "col")),
        check_vma=False,
    )
```

```python
import functools

import jax
import jax.numpy as jnp
from jax import lax
from jax.experimental import pallas as pl
from jax.experimental.pallas import tpu as pltpu
from jax.sharding import PartitionSpec as P

HEAD = 64
CH = 16
PATCH = 2
STEPS = 28
SHIFT_FACTOR = 3.0
EPS = 1e-06
LANES = 128
TORUS = (4, 4, 8)
MESH = pl.DeviceIdType.MESH
F32, BF16 = jnp.float32, jnp.bfloat16


def noise_level(step_number):
    fraction = 1.0 - jnp.full((1, 1), step_number, jnp.int32).astype(F32) / STEPS
    return SHIFT_FACTOR * fraction / (1.0 + (SHIFT_FACTOR - 1.0) * fraction)


def block_kernel(
    torus,
    qkv_hbm, text_hbm, gq_hbm, gk_hbm, gt_hbm, wt_hbm, fw_hbm, hid_hbm, mod_hbm,
    lat_hbm, index_ref, count_ref,
    out_ref,
    qkv, text, hid_in, hid, mod, fw, fw_full, gain_in, gains, block, lat, patch, pixels,
    v_out, k_out, q_out, q_all, k_all, v_all, w_own, w_oth,
    att_out, att_in, att_own, p_oth, base,
    load_sem, send_sem, recv_sem, pair_send, pair_recv, w_send, w_recv,
):
    row, col = lax.axis_index("row"), lax.axis_index("col")
    to_row, to_col = {"row": 1 - row}, {"col": 1 - col}
    tile = qkv.shape[0]
    words = text.shape[0]
    pairs, keys, _ = k_all.shape
    width = pairs * LANES
    half = wt_hbm.shape[0]
    features = w_own.shape[0]

    def load(source, target, at):
        return pltpu.make_async_copy(source, target, load_sem.at[at])

    def remote(source, target, sems, at, device):
        return pltpu.make_async_remote_copy(
            src_ref=source, dst_ref=target, send_sem=sems[0].at[at], recv_sem=sems[1].at[at],
            device_id=device, device_id_type=MESH,
        )

    plain, paired, weight = (send_sem, recv_sem), (pair_send, pair_recv), (w_send, w_recv)

    own_half = pl.ds(pl.multiple_of(row * half, 64), half)
    load_qkv = load(qkv_hbm, qkv, 0)
    load_text = load(text_hbm, text, 1)
    load_w = load(wt_hbm, w_own.at[own_half], 2)
    load_fw = load(fw_hbm, fw.at[row], 3)
    load_hid = load(hid_hbm, hid_in, 4)
    load_mod = load(mod_hbm, mod, 5)
    load_lat = load(lat_hbm, lat, 6)
    load_gains = [load(ref, gain_in.at[at], 7 + at) for at, ref in enumerate((gq_hbm, gk_hbm, gt_hbm))]
    load_qkv.start()
    for copy in load_gains:
        copy.start()

    partners = [to_row, to_col]
    if torus:
        size_x, size_y, size_z = torus
        req = lax.axis_index("req")
        at_z = req % size_z
        at_y = (req // size_z) % size_y
        at_x = req // (size_z * size_y)

        def chip(x, y, z):
            return ((x % size_x) * size_y + y % size_y) * size_z + z % size_z

        to_y = {"req": chip(at_x, at_y + size_y + 2 * col - 1, at_z), "col": 1 - col}
        to_x = [{"req": chip(at_x + step, at_y, at_z)} for step in (1, size_x - 1)]
        partners += [to_y, *to_x]

    barrier = pltpu.get_barrier_semaphore()
    for partner in partners:
        pl.semaphore_signal(barrier, inc=1, device_id=partner, device_id_type=MESH)

    down = lax.broadcasted_iota(jnp.int32, (2 * LANES, LANES), 0) // HEAD
    across = lax.broadcasted_iota(jnp.int32, (2 * LANES, LANES), 1) // HEAD
    block[...] = jnp.where(down % 2 == across, 1.0 / HEAD, 0.0).astype(BF16)

    pl.semaphore_wait(barrier, len(partners))

    if torus:
        quarter = half // 4
        third = quarter // 48 * 16
        parts = ((0, third), (third, quarter - 2 * third), (quarter - third, third))

        def piece(which, part, base):
            start, count = parts[part]
            offset = base + (which % 4) * quarter + start
            return pl.ds(pl.multiple_of(offset, 16), count)

        def near(side, part):
            which = at_x + 2 * side
            return remote(
                wt_hbm.at[piece(which, part, 0)],
                w_oth.at[piece(which, part, row * half)], weight, 2 * side + part, to_y,
            )

        def spread(which, part, at, device):
            rows = piece(which, part, row * half)
            return remote(w_oth.at[rows], w_oth.at[rows], weight, at, device)

        def across_x(part, side, which):
            return spread(which, part, 5 + 3 * side + part, to_x[side])

        def across_two(which):
            return spread(which, 0, 11, to_x[0])

        def across_row(part, away):
            return spread(at_x + away, part, 12 + 3 * away + part, to_row)

        for part in range(3):
            near(0, part).start()
        near(1, 1).start()
        near(1, 2).start()
    else:
        near = remote(wt_hbm, w_oth.at[own_half], weight, 0, to_col)
    w_row = remote(wt_hbm, w_own.at[own_half], plain, 0, to_row)
    fw_row = remote(fw_hbm, fw.at[row], plain, 1, to_row)
    w_row.start()
    fw_row.start()

    def head_norm(values, gain):
        count = values.shape[0]
        pieces = [values[:, LANES * at : LANES * (at + 1)] for at in range(pairs)]
        stacked = jnp.concatenate(pieces, axis=0).astype(F32)
        square = stacked * stacked
        high = square.astype(BF16)
        low = (square - high.astype(F32)).astype(BF16)
        mean = jnp.dot(
            jnp.concatenate([high, low], axis=1), block[...], preferred_element_type=F32
        )
        normed = (stacked * lax.rsqrt(mean + EPS) * gain).astype(BF16)
        return normed.reshape(pairs, count, LANES)

    def split(values):
        return [values[:, LANES * at : LANES * (at + 1)] for at in range(pairs)]

    mine = pl.ds(pl.multiple_of(col * width, LANES), width)
    other = pl.ds(pl.multiple_of((1 - col) * width, LANES), width)
    own_rows, col_rows = pl.ds(0, tile), pl.ds(tile, tile)
    row_rows, far_rows = pl.ds(2 * tile, tile), pl.ds(3 * tile, tile)
    own_text, row_text = pl.ds(4 * tile, words), pl.ds(4 * tile + words, words)

    def k_col(at):
        return remote(k_out.at[at], k_all.at[at, col_rows], paired, at, to_col)

    def v_col(at):
        return remote(v_out.at[at], v_all.at[at, col_rows], paired, pairs + at, to_col)

    def q_col(at):
        return remote(q_out.at[at], q_all.at[at, own_rows], paired, 2 * pairs + at, to_col)

    def k_far(at):
        return remote(
            k_all.at[at, col_rows], k_all.at[at, far_rows], paired, 3 * pairs + at, to_row
        )

    def v_far(at):
        return remote(
            v_all.at[at, col_rows], v_all.at[at, far_rows], paired, 4 * pairs + at, to_row
        )

    def att_col(at):
        return remote(att_out.at[at], att_in.at[at], paired, 5 * pairs + at, to_col)

    load_qkv.wait()
    for copy in (load_text, load_w, load_fw, load_hid, load_mod, load_lat):
        copy.start()
    for at, part in enumerate(split(qkv[:, 2, other])):
        v_out[at] = part
    v_col(0).start()
    v_col(1).start()
    for at, copy in enumerate(load_gains):
        copy.wait()
        gains[at : at + 1, 0:HEAD] = gain_in[at]
        gains[at : at + 1, HEAD:LANES] = gain_in[at]
    k_out[...] = head_norm(qkv[:, 1, other], gains[1:2])
    k_col(0).start()
    q_out[...] = head_norm(qkv[:, 0, other], gains[0:1] * 0.125)
    q_col(0).start()
    k_col(1).start()
    q_col(1).start()
    for at in range(2, pairs):
        k_col(at).start()
        v_col(at).start()
        q_col(at).start()

    for at, part in enumerate(split(qkv[:, 2, mine])):
        v_all[at, own_rows, :] = part
    v_row = remote(v_all.at[:, own_rows], v_all.at[:, row_rows], plain, 2, to_row)
    v_row.start()
    k_all[:, own_rows, :] = head_norm(qkv[:, 1, mine], gains[1:2])
    k_row = remote(k_all.at[:, own_rows], k_all.at[:, row_rows], plain, 3, to_row)
    k_row.start()
    load_text.wait()
    for at, part in enumerate(split(text[:, 1, :])):
        v_all[at, own_text, :] = part
    vt_row = remote(v_all.at[:, own_text], v_all.at[:, row_text], plain, 4, to_row)
    vt_row.start()
    k_all[:, own_text, :] = head_norm(text[:, 0, :], gains[2:3])
    kt_row = remote(k_all.at[:, own_text], k_all.at[:, row_text], plain, 5, to_row)
    kt_row.start()
    if not torus:
        near.start()
    q_all[:, col_rows, :] = head_norm(qkv[:, 0, mine], gains[0:1] * 0.125)

    def spread_near(part):
        near(0, part).wait_recv()
        across_x(part, 0, at_x).start()
        across_x(part, 1, at_x).start()
        across_row(part, 0).start()

    def pass_x(part):
        across_x(part, 0, at_x + 3).wait_recv()
        if part == 0:
            across_two(at_x + 3).start()
        across_row(part, 3).start()
        across_x(part, 1, at_x + 1).wait_recv()
        across_row(part, 1).start()

    def pass_near(part):
        near(1, part).wait_recv()
        across_row(part, 2).start()

    v_row.wait()
    k_row.wait()
    vt_row.wait()
    kt_row.wait()

    low_half = lax.broadcasted_iota(jnp.int32, (tile, LANES), 1) < HEAD
    ones = jnp.ones((keys, LANES), BF16)

    def attend(at, rows):
        pair = q_all[at, rows, :].astype(F32)
        both = jnp.concatenate(
            [jnp.where(low_half, pair, 0.0), jnp.where(low_half, 0.0, pair)], axis=0
        ).astype(BF16)
        scores = lax.dot_general(
            both, k_all[at], (((1,), (1,)), ((), ())), preferred_element_type=F32
        )
        weights = jnp.exp(scores).astype(BF16)
        sums = jnp.dot(
            weights, jnp.concatenate([v_all[at], ones], axis=1), preferred_element_type=F32
        )
        weighted = jnp.where(low_half, sums[:tile, :LANES], sums[tile:, :LANES])
        totals = jnp.where(low_half, sums[:tile, LANES:], sums[tile:, LANES:])
        return (weighted / totals).astype(BF16)

    def attend_pair(at):
        k_far(at).wait_recv()
        v_far(at).wait_recv()
        q_col(at).wait_recv()
        att_out[at] = attend(at, own_rows)
        att_col(at).start()
        att_own[at] = attend(at, col_rows)

    def project(attended, weights, first, last):
        joined = jnp.concatenate([attended[at] for at in range(first, last)], axis=1)
        return lax.dot_general(
            joined, weights[:, LANES * first : LANES * last], (((1,), (1,)), ((), ())),
            preferred_element_type=F32,
        )

    grid_cols = hid_in.shape[1]
    for at in range(pairs):
        k_col(at).wait_recv()
        k_far(at).start()
        v_col(at).wait_recv()
        v_far(at).start()
        if torus and at < 2:
            spread_near(at)
        if torus and at == 3:
            pass_x(0)
        if at > 0:
            attend_pair(at - 1)
        if at == 0:
            load_hid.wait()
            for line in range(hid_in.shape[0]):
                hid[grid_cols * line : grid_cols * (line + 1), :] = hid_in[line]
            load_fw.wait()
            fw_row.wait()
            fw_full[:, 0:half] = fw[0]
            fw_full[:, half:features] = fw[1]
        if torus and at == 2:
            spread_near(2)
        if torus and at == 3:
            pass_x(1)
        if torus and at == 4:
            pass_near(1)
        if at == 3:
            load_w.wait()
            w_row.wait()
            base[...] = project(att_own, w_own, 0, 2)
    attend_pair(pairs - 1)
    if torus:
        pass_x(2)
        pass_near(2)

    rows = tile // 3
    load_mod.wait()
    base[...] += project(att_own, w_own, 2, pairs)

    @pl.loop(0, 3)
    def _(at):
        part = pl.ds(pl.multiple_of(at * rows, 16), rows)
        product = base[part, :].astype(BF16).astype(F32)
        base[part, :] = hid[part, :].astype(F32) + mod[2:3, :] * product

    if torus:
        across_two(at_x + 2).wait_recv()
        across_row(0, 2).start()
        for part in range(3):
            for away in range(4):
                across_row(part, away).wait()
    else:
        near.wait()
        w_far = remote(w_oth.at[own_half], w_oth.at[own_half], weight, 1, to_row)
        w_far.start()
        w_far.wait()
    for at in range(pairs):
        att_col(at).wait_recv()
    p_oth[...] = project(att_in, w_oth, 0, pairs).astype(BF16)

    @pl.loop(0, 3)
    def _(at):
        part = pl.ds(pl.multiple_of(at * rows, 16), rows)
        mixed = base[part, :] + mod[2:3, :] * p_oth[part, :].astype(F32)
        mean = jnp.sum(mixed, axis=-1, keepdims=True) * (1.0 / features)
        centered = mixed - mean
        var = jnp.sum(centered * centered, axis=-1, keepdims=True) * (1.0 / features)
        normed = centered * lax.rsqrt(var + EPS) * (1.0 + mod[1:2, :]) + mod[0:1, :]
        p_oth[part, :] = normed.astype(BF16)

    patch[:, 0:HEAD] = lax.dot_general(
        p_oth[...], fw_full[...], (((1,), (1,)), ((), ())), preferred_element_type=F32
    )

    load_lat.wait()
    span = PATCH * CH
    side = tile // grid_cols
    lane = lax.broadcasted_iota(jnp.int32, (side, LANES), 1) // span
    euler = noise_level(index_ref[0] + count_ref[0]) - noise_level(index_ref[0])
    step = LANES // span
    for first_col in range(0, grid_cols, step):
        columns = [
            patch[pl.ds(first_col + at, side, stride=grid_cols), :] for at in range(step)
        ]
        lanes = slice(first_col * span, (first_col + step) * span)
        for line in range(PATCH):
            merged = jnp.zeros((side, LANES), F32)
            for at, values in enumerate(columns):
                moved = pltpu.roll(values, (at - line) % step * span, 1)
                merged = jnp.where(lane == at, moved, merged)
            pixels[first_col // step, pl.ds(line, side, stride=PATCH), :] = merged
        velocity = pixels[first_col // step]
        out_ref[0, :, lanes] = velocity
        out_ref[1, :, lanes] = lat[:, lanes] + euler * velocity

    for at in range(pairs):
        for copy in (k_col, v_col, q_col, k_far, v_far, att_col):
            copy(at).wait_send()
    if torus:
        across_two(at_x + 3).wait_send()
        near(1, 1).wait_send()
        near(1, 2).wait_send()
        for part in range(3):
            near(0, part).wait_send()
            across_x(part, 0, at_x).wait_send()
            across_x(part, 1, at_x).wait_send()


def on_device(
    torus,
    image_qkv, text_kv, gain_query, gain_key, gain_text, out_weight, final_weight,
    hidden, modulation, latent, step_index, step_count,
):
    tile_rows, tile_cols, _, heads_width = image_qkv.shape
    tile = tile_rows * tile_cols
    words, _, width = text_kv.shape
    half = out_weight.shape[1]
    features = hidden.shape[2]
    patch_values = final_weight.shape[0]
    keys = 4 * tile + 2 * words
    pairs = width // LANES
    anywhere = pl.BlockSpec(memory_space=pltpu.HBM)
    vmem = pl.BlockSpec(memory_space=pltpu.VMEM)
    both = pl.pallas_call(
        functools.partial(block_kernel, torus),
        out_shape=jax.ShapeDtypeStruct((2, *latent.shape), F32),
        in_specs=[anywhere] * 10 + [pl.BlockSpec(memory_space=pltpu.SMEM)] * 2,
        out_specs=vmem,
        scratch_shapes=[
            pltpu.VMEM((tile, 3, heads_width), BF16),
            pltpu.VMEM((words, 2, width), BF16),
            pltpu.VMEM((tile_rows, tile_cols, features), BF16),
            pltpu.VMEM((tile, features), BF16),
            pltpu.VMEM((3, features), F32),
            pltpu.VMEM((2, patch_values, half), BF16),
            pltpu.VMEM((patch_values, features), BF16),
            pltpu.VMEM((3, 1, HEAD), F32),
            pltpu.VMEM((8, LANES), F32),
            pltpu.VMEM((2 * LANES, LANES), BF16),
            pltpu.VMEM(latent.shape, F32),
            pltpu.VMEM((tile, LANES), F32),
            pltpu.VMEM((latent.shape[1] // LANES, latent.shape[0], LANES), F32),
            pltpu.VMEM((pairs, tile, LANES), BF16),
            pltpu.VMEM((pairs, tile, LANES), BF16),
            pltpu.VMEM((pairs, tile, LANES), BF16),
            pltpu.VMEM((pairs, 2 * tile, LANES), BF16),
            pltpu.VMEM((pairs, keys, LANES), BF16),
            pltpu.VMEM((pairs, keys, LANES), BF16),
            pltpu.VMEM((features, width), BF16),
            pltpu.VMEM((features, width), BF16),
            pltpu.VMEM((pairs, tile, LANES), BF16),
            pltpu.VMEM((pairs, tile, LANES), BF16),
            pltpu.VMEM((pairs, tile, LANES), BF16),
            pltpu.VMEM((tile, features), BF16),
            pltpu.VMEM((tile, features), F32),
            pltpu.SemaphoreType.DMA((10,)),
            pltpu.SemaphoreType.DMA((6,)),
            pltpu.SemaphoreType.DMA((6,)),
            pltpu.SemaphoreType.DMA((6 * pairs,)),
            pltpu.SemaphoreType.DMA((6 * pairs,)),
            pltpu.SemaphoreType.DMA((24,)),
            pltpu.SemaphoreType.DMA((24,)),
        ],
        compiler_params=pltpu.CompilerParams(
            collective_id=0, has_side_effects=True, vmem_limit_bytes=40 * 1024 * 1024
        ),
        name="attention_block",
    )(
        *(
            pltpu.with_memory_space_constraint(operand, pltpu.HBM)
            for operand in (
                image_qkv.reshape(tile, 3, heads_width), text_kv,
                gain_query.reshape(1, HEAD), gain_key.reshape(1, HEAD),
                gain_text.reshape(1, HEAD), out_weight.T, final_weight, hidden, modulation,
                latent,
            )
        ),
        step_index, step_count,
    )
    return (both[0], both[1])


def solution(mesh):
    placed = (
        P(("req", "row"), "col", None, None),
        P(("req", "row"), None, "col"),
        P(),
        P(),
        P(),
        P("col", "row"),
        P(None, "row"),
        P(("req", "row"), "col", None),
        P("req", None),
        P(("req", "row"), "col"),
        P("req"),
        P("req"),
    )
    torus = TORUS if mesh.shape["req"] == TORUS[0] * TORUS[1] * TORUS[2] else None
    return jax.shard_map(
        functools.partial(on_device, torus),
        mesh=mesh,
        in_specs=placed,
        out_specs=(P(("req", "row"), "col"), P(("req", "row"), "col")),
        check_vma=False,
    )
```
